256 devices in a mesh: batch: 16 (over z, core), seq: 16 (over y, x).
Axes of the slice: x: 4, y: 4, z: 8, core: 2. Of those that a mesh axis runs over, the one named last changes fastest.
Arguments:
- token_cond: bfloat16 [131072, 768], P(('batch', 'seq')), parts along dimension 0, may hold values from -6 to 6
- atom_feat: bfloat16 [1048576, 128], P(('batch', 'seq')), parts along dimension 0, may hold values from -16 to 16
- atom_counts: int32 [131072], P(('batch', 'seq')), parts along dimension 0, may hold values from 1 to 24, as said below
- w_token: bfloat16 [768, 128], replicated, may hold values from -0.21875 to 0.21875
- w_query: bfloat16 [128, 128], replicated, may hold values from -0.5 to 0.5
- w_key: bfloat16 [128, 128], replicated, may hold values from -0.5 to 0.5
- w_value: bfloat16 [128, 128], replicated, may hold values from -0.5 to 0.5
- w_out: bfloat16 [128, 128], replicated, may hold values from -0.5 to 0.5
- w_back: bfloat16 [128, 768], replicated, may hold values from -0.5 to 0.5
Outputs:
- token_out: bfloat16 [131072, 768], P(('batch', 'seq')), parts along dimension 0
- atom_out: bfloat16 [1048576, 128], P(('batch', 'seq')), parts along dimension 0
The draws below stay inside these ranges and needn't reach their ends.
There are 16 independent parts, one for each index of `batch`. The reference program is written for one: setup_inputs(seed, part) draws one part's arguments, and reference() takes and returns one part's arrays. A program takes and returns all parts, laid end to end along the dimension named above; an argument that names none is the same for every part. Nothing has to cross between parts.
Inputs may be any that keep to these rules, and one draw needn't show every extreme that they name: `atom_counts`: every token has at least one atom and the counts of one complex sum to 65536. For every k, the atoms k * 4096 to (k + 1) * 4096 - 1 belong to tokens of (k - 1) * 512 to (k + 2) * 512 - 1.
All inputs are finite; a program needn't handle non-finite values.
Results may differ from the reference program's by a relative error of at most 0.0095.
The reference program's roundings to bfloat16 on the way count: a program that leaves them out, or rounds other values in their place, can miss the bound.
Values may be sent and summed in bfloat16 or wider, within the bound.
No kernel may reach another device: no remote copies, remote signals or barrier semaphores. Data moves between devices by JAX's collectives and lax.ppermute only.
A program may use at most 128 MiB of HBM per device.

```python
import jax
import jax.numpy as jnp

CT = 768
CA = 128
HEADS = 4
HEAD = 32
QBLOCK = 32
KEYS = 128
MOST = 24
TOK_DEV = 512
ATOM_DEV = 4096
HALO = 48
NTOK = 8192
NATOM = 65536


def draw_atom_feat(key, part):
    first = jax.random.fold_in(jax.random.fold_in(key, 11), 0)
    values = jax.random.normal(first, (NATOM, CA), jnp.float32)
    values = jnp.clip(values, -6.0, 6.0)
    return values.astype(jnp.bfloat16)


def draw_atom_counts(key, part):
    first, second, third, fourth, fifth = jax.random.split(jax.random.fold_in(key, 23), 5)
    nblocks = NTOK // TOK_DEV
    slots = MOST - 1
    magnitude = jax.random.randint(first, (nblocks - 1,), 2 * TOK_DEV, 3 * TOK_DEV + 1)
    flip = jax.random.randint(second, (), 0, 2)
    signs = 1 - 2 * ((jnp.arange(nblocks - 1, dtype=jnp.int32) + flip) % 2)
    drift = jnp.concatenate([jnp.zeros((1,), jnp.int32), (magnitude * signs).astype(jnp.int32), jnp.zeros((1,), jnp.int32)])
    block_sum = ATOM_DEV + drift[1:] - drift[:-1]
    extra = block_sum - TOK_DEV
    levels = jax.random.randint(third, (nblocks, TOK_DEV // 4), 0, 4)
    token_level = jnp.repeat(levels, 4, axis=1)
    widest = jnp.argmax(extra).astype(jnp.int32)
    chosen_token = jax.random.randint(fourth, (), 0, TOK_DEV)
    forced = (jnp.arange(nblocks, dtype=jnp.int32)[:, None] == widest) & (jnp.arange(TOK_DEV, dtype=jnp.int32)[None, :] == chosen_token)
    token_level = jnp.where(forced, 4, token_level)
    noise = jax.random.randint(fifth, (nblocks, TOK_DEV, slots), 0, 4096)
    score = (token_level[:, :, None] * 4096 + noise).reshape(nblocks, TOK_DEV * slots)
    order = jnp.argsort(-score, axis=1, stable=True)
    rank = jnp.argsort(order, axis=1, stable=True)
    taken = (rank < extra[:, None]).astype(jnp.int32)
    counts = 1 + jnp.sum(taken.reshape(nblocks, TOK_DEV, slots), axis=2)
    return counts.reshape(NTOK).astype(jnp.int32)


def shard_levels(rng, dims, shards, low, top_value):
    gain = 1.0
    for dim, parts in shards:
        draws = jax.random.uniform(jax.random.fold_in(jax.random.fold_in(rng, 6), dim), (parts,), jnp.float32, low / len(shards), top_value / len(shards))
        gain = gain * jnp.repeat(jnp.exp(draws), dims[dim] // parts).reshape((-1,) + (1,) * (len(dims) - 1 - dim))
    return gain


def gaussian(rng, extent, width, limit, cuts=(), kind=jnp.bfloat16):
    drawn = width * jax.random.normal(rng, extent, jnp.float32)
    if cuts:
        drawn = drawn * shard_levels(rng, extent, cuts, -0.22, 0.18)
    return jnp.clip(drawn, -limit, limit).astype(kind)


def setup_inputs(seed: int = 0, part: int = 0) -> dict:
    splits = jax.random.split(jax.random.key(seed), 10)
    own_keys = jax.random.split(jax.random.fold_in(splits[9], part), 10)
    return {
        "token_cond": gaussian(own_keys[0], (NTOK, CT), 1.0, 6.0, ((0, 16),)),
        "atom_feat": draw_atom_feat(jax.random.fold_in(jax.random.fold_in(splits[9], part), 71), part),
        "atom_counts": draw_atom_counts(jax.random.fold_in(jax.random.fold_in(splits[9], part), 71), part),
        "w_token": gaussian(splits[3], (CT, CA), CT ** -0.5, 0.21875),
        "w_query": gaussian(splits[4], (CA, CA), CA ** -0.5, 0.5),
        "w_key": gaussian(splits[5], (CA, CA), CA ** -0.5, 0.5),
        "w_value": gaussian(splits[6], (CA, CA), CA ** -0.5, 0.5),
        "w_out": gaussian(splits[7], (CA, CA), CA ** -0.5, 0.5),
        "w_back": gaussian(splits[8], (CA, CT), CA ** -0.5, 0.5),
    }


def reference(token_cond, atom_feat, atom_counts, w_token, w_query, w_key, w_value, w_out, w_back):
    proj = jnp.dot(token_cond, w_token, preferred_element_type=jnp.float32).astype(jnp.bfloat16)
    ends = jnp.cumsum(atom_counts).astype(jnp.int32)
    atom_ids = jnp.arange(NATOM, dtype=jnp.int32)
    owner = jnp.searchsorted(ends, atom_ids, side='right').astype(jnp.int32)
    x = (atom_feat.astype(jnp.float32) + proj[owner].astype(jnp.float32)).astype(jnp.bfloat16)
    query = jnp.dot(x, w_query, preferred_element_type=jnp.float32).astype(jnp.bfloat16)
    keyed = jnp.dot(x, w_key, preferred_element_type=jnp.float32).astype(jnp.bfloat16)
    valued = jnp.dot(x, w_value, preferred_element_type=jnp.float32).astype(jnp.bfloat16)
    blocks = NATOM // QBLOCK
    span = KEYS // QBLOCK
    padk = jnp.pad(keyed, ((HALO, HALO), (0, 0))).reshape(blocks + span - 1, QBLOCK, HEADS, HEAD)
    padv = jnp.pad(valued, ((HALO, HALO), (0, 0))).reshape(blocks + span - 1, QBLOCK, HEADS, HEAD)
    keys = jnp.concatenate([padk[j:j + blocks] for j in range(span)], axis=1)
    values = jnp.concatenate([padv[j:j + blocks] for j in range(span)], axis=1)
    qblocks = query.reshape(blocks, QBLOCK, HEADS, HEAD)
    scores = jnp.einsum('bqhd,bkhd->bhqk', qblocks.astype(jnp.float32), keys.astype(jnp.float32)) / jnp.sqrt(jnp.float32(HEAD))
    key_pos = jnp.arange(blocks, dtype=jnp.int32)[:, None] * QBLOCK + jnp.arange(KEYS, dtype=jnp.int32)[None, :] - HALO
    valid = (key_pos >= 0) & (key_pos < NATOM)
    scores = jnp.where(valid[:, None, None, :], scores, jnp.float32(-1e+30))
    weights = jax.nn.softmax(scores, axis=-1).astype(jnp.bfloat16)
    attended = jnp.einsum('bhqk,bkhd->bqhd', weights.astype(jnp.float32), values.astype(jnp.float32))
    attended = attended.reshape(NATOM, CA).astype(jnp.bfloat16)
    atom_out = (x.astype(jnp.float32) + jnp.dot(attended, w_out, preferred_element_type=jnp.float32)).astype(jnp.bfloat16)
    sums = jax.ops.segment_sum(atom_out.astype(jnp.float32), owner, num_segments=NTOK)
    pooled = (sums / atom_counts.astype(jnp.float32)[:, None]).astype(jnp.bfloat16)
    token_out = (token_cond.astype(jnp.float32) + jnp.dot(pooled, w_back, preferred_element_type=jnp.float32)).astype(jnp.bfloat16)
    return (token_out, atom_out)
```

```python
import math

import jax
import jax.numpy as jnp
from jax import lax
from jax.experimental import pallas as pl
from jax.experimental.pallas import tpu as pltpu
from jax.sharding import PartitionSpec as P

BF16 = jnp.bfloat16
F32 = jnp.float32
HEADS = 4
QBLOCK = 32
KEYS = 128
HALO = 48
LANES = 128
PAD = 64
NT = (((1,), (1,)), ((), ()))
TN = (((0,), (0,)), ((), ()))


def plan_kernel(counts_ref, starts_ref, ends_ref, tiles_ref, spad, epad, *, atoms, pad_chunks, chunks):
    position = lax.axis_index("seq")
    rows = counts_ref.shape[0]
    counts = counts_ref[...].astype(F32)
    exact = counts.astype(BF16)
    up_to = (
        lax.broadcasted_iota(jnp.int32, (LANES, LANES), 0)
        <= lax.broadcasted_iota(jnp.int32, (LANES, LANES), 1)
    )
    within = jnp.dot(exact, up_to.astype(F32).astype(BF16), preferred_element_type=F32)
    before = (
        lax.broadcasted_iota(jnp.int32, (rows, rows), 1)
        < lax.broadcasted_iota(jnp.int32, (rows, rows), 0)
    )
    ahead = jnp.dot(before.astype(F32).astype(BF16), exact, preferred_element_type=F32)
    ends = (within + jnp.sum(ahead, axis=1, keepdims=True)).astype(jnp.int32) - position * atoms
    far = 1 << 24
    spad[0:8, :] = jnp.full((8, LANES), -far, jnp.int32)
    epad[0:8, :] = jnp.full((8, LANES), -far, jnp.int32)
    spad[8 + rows : 16 + rows, :] = jnp.full((8, LANES), far, jnp.int32)
    epad[8 + rows : 16 + rows, :] = jnp.full((8, LANES), far, jnp.int32)
    spad[8 : 8 + rows, :] = ends - counts_ref[...]
    epad[8 : 8 + rows, :] = ends
    first = position * (chunks // 3) - (chunks // 3) - pad_chunks + 8
    near_ends = epad[pl.ds(first, 16), :]
    starts_ref[...] = spad[pl.ds(first, 16), :]
    ends_ref[...] = near_ends
    lane = lax.broadcasted_iota(jnp.int32, (16, LANES), 1)
    row = lax.broadcasted_iota(jnp.int32, (16, LANES), 0)
    tiles = atoms // LANES
    tile_start = jnp.where(lane == tiles, -HALO, lane * LANES)
    tile_start = jnp.where(lane == tiles + 1, atoms, tile_start)
    total = chunks + 2 * pad_chunks
    passed = (near_ends[:, LANES - 1 :] <= tile_start) & (row < total)
    index = jnp.sum(passed.astype(F32), axis=0, keepdims=True).astype(jnp.int32)
    index = jnp.minimum(index, total - 2)
    tiles_ref[...] = jnp.broadcast_to(index, (8, LANES))


def atom_kernel(
    tiles_ref, starts_ref, ends_ref, feat_ref, fleft_ref, fright_ref, far_left_ref, left_ref,
    own_ref, right_ref, far_right_ref, wqkv_ref, wout_ref,
    out_ref, send_a_ref, send_b_ref, mine_ref,
    table, member, xs, qs, ks, vs, os, acc,
    *, atoms, tok, ndev,
):
    position = lax.axis_index("seq")
    tiles = atoms // LANES
    edge = far_left_ref.shape[0]
    zero = jnp.zeros((LANES - edge, LANES), BF16)
    base = LANES
    table[0 : base - edge, :] = zero
    table[base - edge : base, :] = far_left_ref[...]
    table[base : base + tok, :] = left_ref[...]
    table[base + tok : base + 2 * tok, :] = own_ref[...]
    table[base + 2 * tok : base + 3 * tok, :] = right_ref[...]
    table[base + 3 * tok : base + 3 * tok + edge, :] = far_right_ref[...]
    table[base + 3 * tok + edge :, :] = zero

    def members(chunk, first, height):
        ids = lax.broadcasted_iota(jnp.int32, (height, 2 * LANES), 0)
        lo = jnp.concatenate([starts_ref[pl.ds(chunk, 1), :], starts_ref[pl.ds(chunk + 1, 1), :]], axis=1) - first
        hi = jnp.concatenate([ends_ref[pl.ds(chunk, 1), :], ends_ref[pl.ds(chunk + 1, 1), :]], axis=1) - first
        return jnp.where((ids >= lo) & (ids < hi), 1.0, 0.0).astype(BF16)

    def rows_of(chunk, hit):
        window = table[pl.ds(pl.multiple_of(chunk * LANES, LANES), 2 * LANES), :]
        return jnp.dot(hit, window, preferred_element_type=F32)

    def halo_rows(index, first, feat):
        chunk = tiles_ref[0, index]
        got = rows_of(chunk, members(chunk, first, HALO))
        return (feat.astype(F32) + got).astype(BF16)

    xs[0 : PAD - HALO, :] = jnp.zeros((PAD - HALO, LANES), BF16)
    xs[PAD + atoms + HALO :, :] = jnp.zeros((PAD - HALO, LANES), BF16)
    xs[PAD - HALO : PAD, :] = halo_rows(tiles, -HALO, fleft_ref[...])
    xs[PAD + atoms : PAD + atoms + HALO, :] = halo_rows(tiles + 1, atoms, fright_ref[...])

    group = 4

    def gather(i, carry):
        for j in range(group):
            t = i * group + j
            at = pl.multiple_of(t * LANES, LANES)
            chunk = tiles_ref[0, t]
            hit = members(chunk, at, LANES)
            member[pl.ds(at, LANES), :] = hit
            x = feat_ref[pl.ds(at, LANES), :].astype(F32) + rows_of(chunk, hit)
            xs[pl.ds(at + PAD, LANES), :] = x.astype(BF16)
        return carry

    lax.fori_loop(0, tiles // group, gather, 0)

    span = (atoms + 2 * PAD) // 11

    def project(i, carry):
        at = pl.multiple_of(i * span, 128)
        r = jnp.dot(xs[pl.ds(at, span), :], wqkv_ref[...], preferred_element_type=F32).astype(BF16)
        qs[pl.ds(at, span), :] = r[:, :LANES]
        ks[pl.ds(at, span), :] = r[:, LANES : 2 * LANES]
        vs[pl.ds(at, span), :LANES] = r[:, 2 * LANES :]
        vs[pl.ds(at, span), LANES:] = jnp.ones((span, LANES), BF16)
        return carry

    lax.fori_loop(0, 11, project, 0)

    @pl.when(position == 0)
    def _():
        ks[PAD - HALO : PAD, :] = jnp.broadcast_to(ks[PAD : PAD + 1, :].astype(F32), (HALO, LANES)).astype(BF16)
        vs[PAD - HALO : PAD, :] = jnp.zeros((HALO, 2 * LANES), BF16)

    @pl.when(position == ndev - 1)
    def _():
        last = PAD + atoms
        ks[last : last + HALO, :] = jnp.broadcast_to(ks[last - 1 : last, :].astype(F32), (HALO, LANES)).astype(BF16)
        vs[last : last + HALO, :] = jnp.zeros((HALO, 2 * LANES), BF16)

    row_head = lax.broadcasted_iota(jnp.int32, (LANES, LANES), 0) // QBLOCK
    lane_head = lax.broadcasted_iota(jnp.int32, (LANES, LANES), 1) // (LANES // HEADS)
    same = (row_head == lane_head).astype(F32).astype(BF16)
    lanes = lax.broadcasted_iota(jnp.int32, (QBLOCK, LANES), 1) // (LANES // HEADS)
    scale = math.log2(math.e) / math.sqrt(LANES // HEADS)

    def diagonal(full):
        parts = [full[h * QBLOCK : (h + 1) * QBLOCK, :] for h in range(HEADS)]
        out = parts[HEADS - 1]
        for h in range(HEADS - 2, -1, -1):
            out = jnp.where(lanes == h, parts[h], out)
        return out

    per = 8

    def attend(i, carry):
        for j in range(per):
            at = pl.multiple_of((i * per + j) * QBLOCK, QBLOCK)
            q = qs[pl.ds(at + PAD, QBLOCK), :]
            q = jnp.concatenate([q] * HEADS, axis=0) * same
            key = ks[pl.ds(at + PAD - HALO, KEYS), :]
            s = lax.dot_general(q, key, NT, preferred_element_type=F32)
            top = jnp.max(s, axis=1, keepdims=True)
            p = jnp.exp2((s - top) * scale).astype(BF16)
            o = jnp.dot(p, vs[pl.ds(at + PAD - HALO, KEYS), :], preferred_element_type=F32)
            o = diagonal(o[:, :LANES]) / diagonal(o[:, LANES:])
            os[pl.ds(at, QBLOCK), :] = o.astype(BF16)
        return carry

    lax.fori_loop(0, atoms // QBLOCK // per, attend, 0)

    tall = 512

    def finish(i, carry):
        at = pl.multiple_of(i * tall, tall)
        r = jnp.dot(os[pl.ds(at, tall), :], wout_ref[...], preferred_element_type=F32)
        out_ref[pl.ds(at, tall), :] = (xs[pl.ds(at + PAD, tall), :].astype(F32) + r).astype(BF16)
        return carry

    lax.fori_loop(0, atoms // tall, finish, 0)

    acc[...] = jnp.zeros_like(acc)

    def pool(i, carry):
        for j in range(group):
            t = i * group + j
            at = pl.multiple_of(t * LANES, LANES)
            chunk = tiles_ref[0, t]
            part = lax.dot_general(
                member[pl.ds(at, LANES), :], out_ref[pl.ds(at, LANES), :], TN, preferred_element_type=F32
            )
            to = pl.ds(pl.multiple_of(chunk * LANES, LANES), 2 * LANES)
            acc[to, :] = acc[to, :] + part
        return carry

    lax.fori_loop(0, tiles // group, pool, 0)
    odd = lax.rem(position, 2)
    from_a = pl.multiple_of(base + (1 - odd) * 2 * tok, LANES)
    from_b = pl.multiple_of(base + odd * 2 * tok, LANES)
    send_a_ref[...] = acc[pl.ds(from_a, tok), :].astype(BF16)
    send_b_ref[...] = acc[pl.ds(from_b, tok), :].astype(BF16)
    mine_ref[...] = acc[base + tok : base + 2 * tok, :]


def shards(token_cond, atom_feat, atom_counts, w_token, w_query, w_key, w_value, w_out, w_back):
    tok = token_cond.shape[0]
    atoms, width = atom_feat.shape
    ndev = lax.axis_size("seq")

    def shifted(x, by):
        return lax.ppermute(x, "seq", [(i, (i + by) % ndev) for i in range(ndev)])

    counts = atom_counts.reshape(tok // LANES, LANES)
    copies = jnp.broadcast_to(counts, (ndev, *counts.shape))
    counts_all = lax.all_to_all(copies, "seq", split_axis=0, concat_axis=0, tiled=True)
    counts_all = counts_all.reshape(ndev * counts.shape[0], LANES)

    proj = jnp.dot(token_cond, w_token, preferred_element_type=F32).astype(BF16)
    from_left = shifted(jnp.concatenate([proj, atom_feat[atoms - HALO :]]), 1)
    from_right = shifted(jnp.concatenate([proj, atom_feat[:HALO]]), -1)
    far_left = shifted(proj[tok - HALO :], 2)
    far_right = shifted(proj[:HALO], -2)

    chunks = 3 * tok // LANES
    near = jax.ShapeDtypeStruct((16, LANES), jnp.int32)
    starts, ends, tiles = pl.pallas_call(
        lambda *refs: plan_kernel(*refs, atoms=atoms, pad_chunks=1, chunks=chunks),
        out_shape=(near, near, jax.ShapeDtypeStruct((8, LANES), jnp.int32)),
        scratch_shapes=[pltpu.VMEM((counts_all.shape[0] + 16, LANES), jnp.int32)] * 2,
        name="plan",
    )(counts_all)

    wqkv = jnp.concatenate([w_query, w_key, w_value], axis=1)
    vmem = pl.BlockSpec(memory_space=pltpu.VMEM)
    total = atoms + 2 * PAD
    window = jax.ShapeDtypeStruct((tok, width), BF16)
    atom_out, send_a, send_b, mine = pl.pallas_call(
        lambda *refs: atom_kernel(*refs, atoms=atoms, tok=tok, ndev=ndev),
        in_specs=[pl.BlockSpec(memory_space=pltpu.SMEM)] + [vmem] * 12,
        out_specs=[vmem] * 4,
        out_shape=(
            jax.ShapeDtypeStruct((atoms, width), BF16),
            window,
            window,
            jax.ShapeDtypeStruct((tok, width), F32),
        ),
        scratch_shapes=[
            pltpu.VMEM((3 * tok + 2 * LANES, width), BF16),
            pltpu.VMEM((atoms, 2 * LANES), BF16),
            pltpu.VMEM((total, width), BF16),
            pltpu.VMEM((total, width), BF16),
            pltpu.VMEM((total, width), BF16),
            pltpu.VMEM((total, 2 * width), BF16),
            pltpu.VMEM((atoms, width), BF16),
            pltpu.VMEM((3 * tok + 2 * LANES, width), F32),
        ],
        compiler_params=pltpu.CompilerParams(vmem_limit_bytes=40 << 20),
        name="atoms",
    )(
        tiles, starts, ends, atom_feat, from_left[tok:], from_right[tok:], far_left, from_left[:tok],
        proj, from_right[:tok], far_right, wqkv, w_out,
    )

    got_a = lax.ppermute(send_a, "seq", [(i, i ^ 1) for i in range(ndev)])
    got_b = lax.ppermute(send_b, "seq", [(i, ((i + 1) ^ 1) - 1) for i in range(1, ndev - 1)])
    sums = mine + got_a.astype(F32) + got_b.astype(F32)
    pooled = (sums / atom_counts.astype(F32)[:, None]).astype(BF16)
    token_out = (
        token_cond.astype(F32) + jnp.dot(pooled, w_back, preferred_element_type=F32)
    ).astype(BF16)
    return (token_out, atom_out)


def solution(mesh):
    whole = P()
    rows = P(("batch", "seq"), None)
    in_specs = (rows, rows, P(("batch", "seq")), whole, whole, whole, whole, whole, whole)
    return jax.shard_map(shards, mesh=mesh, in_specs=in_specs, out_specs=(rows, rows), check_vma=False)
```

```python
import math

import jax
import jax.numpy as jnp
from jax import lax
from jax.experimental import pallas as pl
from jax.experimental.pallas import tpu as pltpu
from jax.sharding import PartitionSpec as P

BF16 = jnp.bfloat16
F32 = jnp.float32
HEADS = 4
QBLOCK = 32
KEYS = 128
HALO = 48
LANES = 128
ONES = 16
PAD = 64
NT = (((1,), (1,)), ((), ()))
TN = (((0,), (0,)), ((), ()))


def plan_kernel(counts_ref, near_ref, far_ref, spad, epad, *, atoms, pad_chunks, chunks):
    position = lax.axis_index("seq")
    rows = counts_ref.shape[0]
    counts = counts_ref[...].astype(F32)
    exact = counts.astype(BF16)
    up_to = (
        lax.broadcasted_iota(jnp.int32, (LANES, LANES), 0)
        <= lax.broadcasted_iota(jnp.int32, (LANES, LANES), 1)
    )
    within = jnp.dot(exact, up_to.astype(F32).astype(BF16), preferred_element_type=F32)
    before = (
        lax.broadcasted_iota(jnp.int32, (rows, rows), 1)
        < lax.broadcasted_iota(jnp.int32, (rows, rows), 0)
    )
    ahead = jnp.dot(before.astype(F32).astype(BF16), exact, preferred_element_type=F32)
    ends = (within + jnp.sum(ahead, axis=1, keepdims=True)).astype(jnp.int32) - position * atoms
    row = lax.broadcasted_iota(jnp.int32, (rows, LANES), 0) + 1
    lane = lax.broadcasted_iota(jnp.int32, (rows, LANES), 1)
    per_dev = chunks // 3
    drift = ends + position * atoms - row // per_dev * atoms
    closes = (row % per_dev == 0) & (lane == LANES - 1)
    wide = jnp.where(closes & (jnp.abs(drift) > atoms - HALO), 1.0, 0.0)
    far_ref[0, 0] = jnp.max(wide).astype(jnp.int32)
    far = 1 << 24
    spad[0:8, :] = jnp.full((8, LANES), -far, jnp.int32)
    epad[0:8, :] = jnp.full((8, LANES), -far, jnp.int32)
    spad[8 + rows : 16 + rows, :] = jnp.full((8, LANES), far, jnp.int32)
    epad[8 + rows : 16 + rows, :] = jnp.full((8, LANES), far, jnp.int32)
    spad[8 : 8 + rows, :] = ends - counts_ref[...]
    epad[8 : 8 + rows, :] = ends
    first = position * (chunks // 3) - (chunks // 3) - pad_chunks + 8
    near_ends = epad[pl.ds(first, 16), :]
    near_ref[8:24, :] = spad[pl.ds(first, 16), :]
    near_ref[24:, :] = near_ends
    lane = lax.broadcasted_iota(jnp.int32, (16, LANES), 1)
    row = lax.broadcasted_iota(jnp.int32, (16, LANES), 0)
    tiles = atoms // LANES
    tile_start = jnp.where(lane == tiles, -HALO, lane * LANES)
    tile_start = jnp.where(lane == tiles + 1, atoms, tile_start)
    total = chunks + 2 * pad_chunks
    passed = (near_ends[:, LANES - 1 :] <= tile_start) & (row < total)
    index = jnp.sum(passed.astype(F32), axis=0, keepdims=True).astype(jnp.int32)
    index = jnp.minimum(index, total - 2)
    near_ref[:8, :] = jnp.broadcast_to(index, (8, LANES))


def atom_kernel(
    tiles_ref, near_ref, feat_ref, left_ref, own_ref, right_ref, far_ref,
    wq_ref, wk_ref, wv_ref, wout_ref,
    out_ref, send_a_ref, send_b_ref, mine_ref,
    table, member, xs, qx, ks, vs, os, acc,
    *, atoms, tok, ndev,
):
    position = lax.axis_index("seq")
    tiles = atoms // LANES
    edge = far_ref.shape[0] // 2
    zero = jnp.zeros((LANES - edge, LANES), BF16)
    base = LANES
    table[0 : base - edge, :] = zero
    table[base - edge : base, :] = far_ref[:edge, :]
    table[base : base + tok, :] = left_ref[:tok, :]
    table[base + tok : base + 2 * tok, :] = own_ref[...]
    table[base + 2 * tok : base + 3 * tok, :] = right_ref[:tok, :]
    table[base + 3 * tok : base + 3 * tok + edge, :] = far_ref[edge:, :]
    table[base + 3 * tok + edge :, :] = zero

    def members(chunk, first, height):
        ids = lax.broadcasted_iota(jnp.int32, (height, 2 * LANES), 0)
        lo = jnp.concatenate([near_ref[pl.ds(chunk + 8, 1), :], near_ref[pl.ds(chunk + 9, 1), :]], axis=1) - first
        hi = jnp.concatenate([near_ref[pl.ds(chunk + 24, 1), :], near_ref[pl.ds(chunk + 25, 1), :]], axis=1) - first
        return jnp.where((ids >= lo) & (ids < hi), 1.0, 0.0).astype(BF16)

    def rows_of(chunk, hit):
        window = table[pl.ds(pl.multiple_of(chunk * LANES, LANES), 2 * LANES), :]
        return jnp.dot(hit, window, preferred_element_type=F32)

    def halo_rows(index, first, feat):
        chunk = tiles_ref[0, index]
        got = rows_of(chunk, members(chunk, first, HALO))
        return (feat.astype(F32) + got).astype(BF16)

    xs[0 : PAD - HALO, :] = jnp.zeros((PAD - HALO, LANES), BF16)
    xs[PAD + atoms + HALO :, :] = jnp.zeros((PAD - HALO, LANES), BF16)
    xs[PAD - HALO : PAD, :] = halo_rows(tiles, -HALO, left_ref[tok + PAD - HALO :, :])
    xs[PAD + atoms : PAD + atoms + HALO, :] = halo_rows(tiles + 1, atoms, right_ref[tok : tok + HALO, :])

    group = 16
    pgroup = 16

    def gather(i, carry):
        for j in range(group):
            t = i * group + j
            at = pl.multiple_of(t * LANES, LANES)
            chunk = tiles_ref[0, t]
            hit = members(chunk, at, LANES)
            member[pl.ds(at, LANES), :] = hit
            x = feat_ref[pl.ds(at, LANES), :].astype(F32) + rows_of(chunk, hit)
            xs[pl.ds(at + PAD, LANES), :] = x.astype(BF16)
        return carry

    lax.fori_loop(0, tiles // group, gather, 0)

    steps = 1
    span = (atoms + 2 * PAD) // steps
    broad = 4096
    wqt = wq_ref[...].T
    wvt = wv_ref[...].T

    def project(i, carry):
        at = pl.multiple_of(i * span, LANES)
        x = xs[pl.ds(at, span), :]
        ks[pl.ds(at, span), :] = jnp.dot(x, wk_ref[...], preferred_element_type=F32).astype(BF16)
        r = lax.dot_general(wvt, x, NT, preferred_element_type=F32).astype(BF16)
        vs[:LANES, pl.ds(at, span)] = r
        vs[LANES:, pl.ds(at, span)] = jnp.ones((ONES, span), BF16)
        return carry

    def turned(x, h):
        return pltpu.roll(x, h * QBLOCK % LANES, 1) if h % HEADS else x

    def ask(i, carry):
        at = pl.multiple_of(i * broad, LANES)
        r = lax.dot_general(wqt, xs[pl.ds(at + PAD, broad), :], NT, preferred_element_type=F32).astype(BF16)
        for c in range(broad // LANES):
            for h in range(HEADS):
                part = r[h * QBLOCK : (h + 1) * QBLOCK, c * LANES : (c + 1) * LANES]
                qx[h * QBLOCK : (h + 1) * QBLOCK, pl.ds(at + c * LANES, LANES)] = turned(part, h)
        return carry

    lax.fori_loop(0, steps, project, 0)
    lax.fori_loop(0, atoms // broad, ask, 0)

    lane = lax.broadcasted_iota(jnp.int32, vs.shape[:1] + (LANES,), 1)

    @pl.when(position == 0)
    def _():
        ks[PAD - HALO : PAD, :] = jnp.broadcast_to(ks[PAD : PAD + 1, :].astype(F32), (HALO, LANES)).astype(BF16)
        vs[:, :LANES] = jnp.where(lane < PAD, 0.0, vs[:, :LANES].astype(F32)).astype(BF16)

    @pl.when(position == ndev - 1)
    def _():
        last = PAD + atoms
        ks[last : last + HALO, :] = jnp.broadcast_to(ks[last - 1 : last, :].astype(F32), (HALO, LANES)).astype(BF16)
        vs[:, atoms:] = jnp.where(lane >= PAD, 0.0, vs[:, atoms:].astype(F32)).astype(BF16)

    head = LANES // HEADS
    scale = math.log2(math.e) / math.sqrt(head)
    row_group = lax.broadcasted_iota(jnp.int32, (LANES, LANES), 0) // head
    lane_group = lax.broadcasted_iota(jnp.int32, (LANES, LANES), 1) // QBLOCK
    kept = [((row_group + j) % HEADS == lane_group).astype(F32).astype(BF16) for j in range(4)]
    group_of = lax.broadcasted_iota(jnp.int32, (head, LANES), 1) // QBLOCK
    blank = jnp.zeros((LANES, LANES), BF16)

    per = 4

    def attend(i, carry):
        for n in range(per):
            at = pl.multiple_of((i * per + n) * LANES, LANES)
            q = qx[:, pl.ds(at, LANES)]
            value = vs[:, pl.ds(at, 2 * LANES)]
            parts = []
            for j in (0, 2):
                key = [ks[pl.ds(at + PAD - HALO + (j + c) * QBLOCK, KEYS), :] for c in range(2)]
                ask_for = jnp.concatenate(
                    [
                        jnp.concatenate([q * kept[j], blank], axis=1),
                        jnp.concatenate([blank, q * kept[j + 1]], axis=1),
                    ],
                    axis=0,
                )
                s = jnp.dot(jnp.concatenate(key, axis=1), ask_for, preferred_element_type=F32)
                top = jnp.max(s, axis=0, keepdims=True)
                p = jnp.exp2((s - top) * scale).astype(BF16)
                cols = []
                for c in range(2):
                    above = PAD - HALO + (j + c) * QBLOCK
                    cols.append(
                        jnp.concatenate(
                            [
                                jnp.zeros((above, LANES), BF16),
                                p[:, c * LANES : (c + 1) * LANES],
                                jnp.zeros((LANES - above, LANES), BF16),
                            ],
                            axis=0,
                        )
                    )
                o = jnp.dot(value, jnp.concatenate(cols, axis=1), preferred_element_type=F32)
                parts += [o[:, :LANES], o[:, LANES:]]
            for h in range(HEADS):
                o = parts[0][h * head : (h + 1) * head, :]
                total = parts[0][LANES : LANES + 1, :]
                for j in range(1, 4):
                    here = group_of == (h + j) % HEADS
                    o = jnp.where(here, parts[j][h * head : (h + 1) * head, :], o)
                    total = jnp.where(here[:1], parts[j][LANES : LANES + 1, :], total)
                o = (o * (1.0 / total)).astype(BF16)
                os[h * head : (h + 1) * head, pl.ds(at, LANES)] = turned(o, -h % HEADS)
        return carry

    lax.fori_loop(0, atoms // LANES // per, attend, 0)

    tall = 4096

    def finish(i, carry):
        at = pl.multiple_of(i * tall, tall)
        r = lax.dot_general(os[:, pl.ds(at, tall)], wout_ref[...], TN, preferred_element_type=F32)
        out_ref[pl.ds(at, tall), :] = (xs[pl.ds(at + PAD, tall), :].astype(F32) + r).astype(BF16)
        return carry

    lax.fori_loop(0, atoms // tall, finish, 0)

    acc[...] = jnp.zeros_like(acc)

    def pool(i, carry):
        for j in range(pgroup):
            t = i * pgroup + j
            at = pl.multiple_of(t * LANES, LANES)
            chunk = tiles_ref[0, t]
            part = lax.dot_general(
                out_ref[pl.ds(at, LANES), :], member[pl.ds(at, LANES), :], TN, preferred_element_type=F32
            )
            to = pl.ds(pl.multiple_of(chunk * LANES, LANES), 2 * LANES)
            acc[:, to] = acc[:, to] + part
        return carry

    lax.fori_loop(0, tiles // pgroup, pool, 0)
    odd = lax.rem(position, 2)
    from_a = pl.multiple_of(base + (1 - odd) * 2 * tok, LANES)
    from_b = pl.multiple_of(base + odd * 2 * tok, LANES)
    send_a_ref[...] = acc[:, pl.ds(from_a, tok)].astype(BF16)
    send_b_ref[...] = acc[:, pl.ds(from_b, tok)].astype(BF16)
    mine_ref[...] = acc[:, base + tok : base + 2 * tok]


def shards(token_cond, atom_feat, atom_counts, w_token, w_query, w_key, w_value, w_out, w_back):
    tok = token_cond.shape[0]
    atoms, width = atom_feat.shape
    ndev = lax.axis_size("seq")

    def shifted(x, by):
        return lax.ppermute(x, "seq", [(i, (i + by) % ndev) for i in range(ndev)])

    counts = atom_counts.reshape(tok // LANES, LANES)
    copies = jnp.broadcast_to(counts, (ndev, *counts.shape))
    counts_all = lax.all_to_all(copies, "seq", split_axis=0, concat_axis=0, tiled=True)
    counts_all = counts_all.reshape(ndev * counts.shape[0], LANES)

    proj = jnp.dot(token_cond, w_token, preferred_element_type=F32).astype(BF16)
    from_left = shifted(jnp.concatenate([proj, atom_feat[atoms - PAD :]]), 1)
    from_right = shifted(jnp.concatenate([proj, atom_feat[:PAD]]), -1)
    whole = pl.BlockSpec(memory_space=pltpu.VMEM)

    chunks = 3 * tok // LANES
    near, far = pl.pallas_call(
        lambda *refs: plan_kernel(*refs, atoms=atoms, pad_chunks=1, chunks=chunks),
        out_shape=(
            jax.ShapeDtypeStruct((40, LANES), jnp.int32),
            jax.ShapeDtypeStruct((1, 1), jnp.int32),
        ),
        in_specs=[whole],
        out_specs=[whole] + [pl.BlockSpec(memory_space=pltpu.SMEM)],
        scratch_shapes=[pltpu.VMEM((counts_all.shape[0] + 16, LANES), jnp.int32)] * 2,
        name="plan",
    )(counts_all)

    beyond = lax.cond(
        far[0, 0] > 0,
        lambda x: jnp.concatenate([shifted(x[tok - HALO :], 2), shifted(x[:HALO], -2)]),
        lambda x: jnp.zeros((2 * HALO, width), BF16),
        proj,
    )
    vmem = whole
    total = atoms + 2 * PAD
    window = jax.ShapeDtypeStruct((width, tok), BF16)
    atom_out, send_a, send_b, mine = pl.pallas_call(
        lambda *refs: atom_kernel(*refs, atoms=atoms, tok=tok, ndev=ndev),
        in_specs=[pl.BlockSpec(memory_space=pltpu.SMEM)] + [vmem] * 10,
        out_specs=[vmem] * 4,
        out_shape=(
            jax.ShapeDtypeStruct((atoms, width), BF16),
            window,
            window,
            jax.ShapeDtypeStruct((width, tok), F32),
        ),
        scratch_shapes=[
            pltpu.VMEM((3 * tok + 2 * LANES, width), BF16),
            pltpu.VMEM((atoms, 2 * LANES), BF16),
            pltpu.VMEM((total, width), BF16),
            pltpu.VMEM((width, atoms), BF16),
            pltpu.VMEM((total, width), BF16),
            pltpu.VMEM((width + ONES, total), BF16),
            pltpu.VMEM((width, atoms), BF16),
            pltpu.VMEM((width, 3 * tok + 2 * LANES), F32),
        ],
        compiler_params=pltpu.CompilerParams(vmem_limit_bytes=40 << 20),
        name="atoms",
    )(
        near, near, atom_feat, from_left, proj, from_right, beyond, w_query, w_key, w_value, w_out,
    )

    got_a = lax.ppermute(send_a, "seq", [(i, i ^ 1) for i in range(ndev)])
    got_b = lax.ppermute(send_b, "seq", [(i, ((i + 1) ^ 1) - 1) for i in range(1, ndev - 1)])
    sums = mine + got_a.astype(F32) + got_b.astype(F32)
    pooled = (sums / atom_counts.astype(F32)[None, :]).astype(BF16)
    token_out = (
        token_cond.astype(F32) + lax.dot_general(pooled, w_back, TN, preferred_element_type=F32)
    ).astype(BF16)
    return (token_out, atom_out)


def solution(mesh):
    whole = P()
    rows = P(("batch", "seq"), None)
    in_specs = (rows, rows, P(("batch", "seq")), whole, whole, whole, whole, whole, whole)
    return jax.shard_map(shards, mesh=mesh, in_specs=in_specs, out_specs=(rows, rows), check_vma=False)
```

```python
import math

import jax
import jax.numpy as jnp
from jax import lax
from jax.experimental import pallas as pl
from jax.experimental.pallas import tpu as pltpu
from jax.sharding import PartitionSpec as P

BF16 = jnp.bfloat16
F32 = jnp.float32
HEADS = 4
QBLOCK = 32
KEYS = 128
HALO = 48
LANES = 128
ONES = 16
PAD = 64
NT = (((1,), (1,)), ((), ()))
TN = (((0,), (0,)), ((), ()))


def plan_kernel(counts_ref, near_ref, far_ref, spad, epad, *, atoms, pad_chunks, chunks):
    position = lax.axis_index("seq")
    rows = counts_ref.shape[0]
    counts = counts_ref[...].astype(F32)
    exact = counts.astype(BF16)
    up_to = (
        lax.broadcasted_iota(jnp.int32, (LANES, LANES), 0)
        <= lax.broadcasted_iota(jnp.int32, (LANES, LANES), 1)
    )
    within = jnp.dot(exact, up_to.astype(F32).astype(BF16), preferred_element_type=F32)
    before = (
        lax.broadcasted_iota(jnp.int32, (rows, rows), 1)
        < lax.broadcasted_iota(jnp.int32, (rows, rows), 0)
    )
    ahead = jnp.dot(before.astype(F32).astype(BF16), exact, preferred_element_type=F32)
    ends = (within + jnp.sum(ahead, axis=1, keepdims=True)).astype(jnp.int32) - position * atoms
    row = lax.broadcasted_iota(jnp.int32, (rows, LANES), 0) + 1
    lane = lax.broadcasted_iota(jnp.int32, (rows, LANES), 1)
    per_dev = chunks // 3
    drift = ends + position * atoms - row // per_dev * atoms
    closes = (row % per_dev == 0) & (lane == LANES - 1)
    wide = jnp.where(closes & (jnp.abs(drift) > atoms - HALO), 1.0, 0.0)
    far_ref[0, 0] = jnp.max(wide).astype(jnp.int32)
    far = 1 << 24
    spad[0:8, :] = jnp.full((8, LANES), -far, jnp.int32)
    epad[0:8, :] = jnp.full((8, LANES), -far, jnp.int32)
    spad[8 + rows : 16 + rows, :] = jnp.full((8, LANES), far, jnp.int32)
    epad[8 + rows : 16 + rows, :] = jnp.full((8, LANES), far, jnp.int32)
    spad[8 : 8 + rows, :] = ends - counts_ref[...]
    epad[8 : 8 + rows, :] = ends
    first = position * (chunks // 3) - (chunks // 3) - pad_chunks + 8
    near_ends = epad[pl.ds(first, 16), :]
    near_ref[8:24, :] = spad[pl.ds(first, 16), :]
    near_ref[24:, :] = near_ends
    lane = lax.broadcasted_iota(jnp.int32, (16, LANES), 1)
    row = lax.broadcasted_iota(jnp.int32, (16, LANES), 0)
    tiles = atoms // LANES
    tile_start = jnp.where(lane == tiles, -HALO, lane * LANES)
    tile_start = jnp.where(lane == tiles + 1, atoms, tile_start)
    total = chunks + 2 * pad_chunks
    passed = (near_ends[:, LANES - 1 :] <= tile_start) & (row < total)
    index = jnp.sum(passed.astype(F32), axis=0, keepdims=True).astype(jnp.int32)
    index = jnp.minimum(index, total - 2)
    near_ref[:8, :] = jnp.broadcast_to(index, (8, LANES))


def atom_kernel(
    tiles_ref, near_hbm, feat_ref, near_a_ref, own_ref, near_b_ref, far_ref,
    wq_ref, wk_ref, wv_ref, wout_ref,
    out_ref, send_a_ref, send_b_ref, mine_ref,
    table, member, xs, qx, ks, vs, os, acc, near_ref, near_sem,
    *, atoms, tok, ndev,
):
    position = lax.axis_index("seq")
    arrive = pltpu.make_async_copy(near_hbm, near_ref, near_sem)
    arrive.start()
    tiles = atoms // LANES
    edge = far_ref.shape[0] // 2
    zero = jnp.zeros((LANES - edge, LANES), BF16)
    base = LANES
    table[0 : base - edge, :] = zero
    table[base - edge : base, :] = far_ref[:edge, :]
    odd = lax.rem(position, 2)
    from_a = pl.multiple_of(base + (1 - odd) * 2 * tok, LANES)
    from_b = pl.multiple_of(base + odd * 2 * tok, LANES)
    table[pl.ds(from_a, tok), :] = near_a_ref[:tok, :]
    table[pl.ds(from_b, tok), :] = near_b_ref[:tok, :]
    table[base + tok : base + 2 * tok, :] = own_ref[...]
    table[base + 3 * tok : base + 3 * tok + edge, :] = far_ref[edge:, :]
    table[base + 3 * tok + edge :, :] = zero

    def members(chunk, first, height):
        ids = lax.broadcasted_iota(jnp.int32, (height, 2 * LANES), 0)
        lo = jnp.concatenate([near_ref[pl.ds(chunk + 8, 1), :], near_ref[pl.ds(chunk + 9, 1), :]], axis=1) - first
        hi = jnp.concatenate([near_ref[pl.ds(chunk + 24, 1), :], near_ref[pl.ds(chunk + 25, 1), :]], axis=1) - first
        return jnp.where((ids >= lo) & (ids < hi), 1.0, 0.0).astype(BF16)

    def rows_of(chunk, hit):
        window = table[pl.ds(pl.multiple_of(chunk * LANES, LANES), 2 * LANES), :]
        return jnp.dot(hit, window, preferred_element_type=F32)

    def halo_rows(index, first, feat):
        chunk = tiles_ref[0, index]
        got = rows_of(chunk, members(chunk, first, HALO))
        return (feat.astype(F32) + got).astype(BF16)

    is_odd = jnp.full((HALO, LANES), odd, jnp.int32) == 1
    before = slice(tok + 2 * PAD - HALO, tok + 2 * PAD)
    after = slice(tok, tok + HALO)
    arrive.wait()
    xs[0 : PAD - HALO, :] = jnp.zeros((PAD - HALO, LANES), BF16)
    xs[PAD + atoms + HALO :, :] = jnp.zeros((PAD - HALO, LANES), BF16)
    xs[PAD - HALO : PAD, :] = halo_rows(tiles, -HALO, jnp.where(is_odd, near_a_ref[before, :].astype(F32), near_b_ref[before, :].astype(F32)))
    xs[PAD + atoms : PAD + atoms + HALO, :] = halo_rows(tiles + 1, atoms, jnp.where(is_odd, near_b_ref[after, :].astype(F32), near_a_ref[after, :].astype(F32)))

    group = 32
    pgroup = 32

    def gather(i, carry):
        first = [pl.multiple_of((i * group + j) * LANES, LANES) for j in range(group)]
        chunk = [tiles_ref[0, i * group + j] for j in range(group)]
        hits = [members(c, at, LANES) for c, at in zip(chunk, first)]
        got = [rows_of(c, hit) for c, hit in zip(chunk, hits)]
        for at, hit, rows in zip(first, hits, got):
            member[pl.ds(at, LANES), :] = hit
            x = feat_ref[pl.ds(at, LANES), :].astype(F32) + rows
            xs[pl.ds(at + PAD, LANES), :] = x.astype(BF16)
        return carry

    lax.fori_loop(0, tiles // group, gather, 0)

    steps = 1
    span = (atoms + 2 * PAD) // steps
    broad = 4096
    wqt = wq_ref[...].T
    wvt = wv_ref[...].T

    def project(i, carry):
        at = pl.multiple_of(i * span, LANES)
        x = xs[pl.ds(at, span), :]
        ks[pl.ds(at, span), :] = jnp.dot(x, wk_ref[...], preferred_element_type=F32).astype(BF16)
        r = lax.dot_general(wvt, x, NT, preferred_element_type=F32).astype(BF16)
        vs[:LANES, pl.ds(at, span)] = r
        vs[LANES:, pl.ds(at, span)] = jnp.ones((ONES, span), BF16)
        return carry

    def turned(x, h):
        return pltpu.roll(x, h * QBLOCK % LANES, 1) if h % HEADS else x

    def ask(i, carry):
        at = pl.multiple_of(i * broad, LANES)
        r = lax.dot_general(wqt, xs[pl.ds(at + PAD, broad), :], NT, preferred_element_type=F32).astype(BF16)
        for c in range(broad // LANES):
            for h in range(HEADS):
                part = r[h * QBLOCK : (h + 1) * QBLOCK, c * LANES : (c + 1) * LANES]
                qx[h * QBLOCK : (h + 1) * QBLOCK, pl.ds(at + c * LANES, LANES)] = turned(part, h)
        return carry

    lax.fori_loop(0, steps, project, 0)
    lax.fori_loop(0, atoms // broad, ask, 0)

    lane = lax.broadcasted_iota(jnp.int32, vs.shape[:1] + (LANES,), 1)

    @pl.when(position == 0)
    def _():
        ks[PAD - HALO : PAD, :] = jnp.broadcast_to(ks[PAD : PAD + 1, :].astype(F32), (HALO, LANES)).astype(BF16)
        vs[:, :LANES] = jnp.where(lane < PAD, 0.0, vs[:, :LANES].astype(F32)).astype(BF16)

    @pl.when(position == ndev - 1)
    def _():
        last = PAD + atoms
        ks[last : last + HALO, :] = jnp.broadcast_to(ks[last - 1 : last, :].astype(F32), (HALO, LANES)).astype(BF16)
        vs[:, atoms:] = jnp.where(lane >= PAD, 0.0, vs[:, atoms:].astype(F32)).astype(BF16)

    head = LANES // HEADS
    scale = math.log2(math.e) / math.sqrt(head)
    row_group = lax.broadcasted_iota(jnp.int32, (LANES, LANES), 0) // head
    lane_group = lax.broadcasted_iota(jnp.int32, (LANES, LANES), 1) // QBLOCK
    kept = [((row_group + j) % HEADS == lane_group).astype(F32).astype(BF16) for j in range(4)]
    group_of = lax.broadcasted_iota(jnp.int32, (head, LANES), 1) // QBLOCK
    blank = jnp.zeros((LANES, LANES), BF16)

    per = 32

    def attend(i, carry):
        asked, weighed, summed = [], [], []
        for n in range(per):
            at = pl.multiple_of((i * per + n) * LANES, LANES)
            q = qx[:, pl.ds(at, LANES)]
            for j in (0, 2):
                key = [ks[pl.ds(at + PAD - HALO + (j + c) * QBLOCK, KEYS), :] for c in range(2)]
                ask_for = jnp.concatenate(
                    [
                        jnp.concatenate([q * kept[j], blank], axis=1),
                        jnp.concatenate([blank, q * kept[j + 1]], axis=1),
                    ],
                    axis=0,
                )
                asked.append(jnp.dot(jnp.concatenate(key, axis=1), ask_for, preferred_element_type=F32))
        for s in asked:
            top = jnp.max(s, axis=0, keepdims=True)
            weighed.append(jnp.exp2((s - top) * scale).astype(BF16))
        for n in range(per):
            at = pl.multiple_of((i * per + n) * LANES, LANES)
            value = vs[:, pl.ds(at, 2 * LANES)]
            for j in (0, 2):
                p = weighed[2 * n + j // 2]
                cols = []
                for c in range(2):
                    above = PAD - HALO + (j + c) * QBLOCK
                    cols.append(
                        jnp.concatenate(
                            [
                                jnp.zeros((above, LANES), BF16),
                                p[:, c * LANES : (c + 1) * LANES],
                                jnp.zeros((LANES - above, LANES), BF16),
                            ],
                            axis=0,
                        )
                    )
                summed.append(jnp.dot(value, jnp.concatenate(cols, axis=1), preferred_element_type=F32))
        for n in range(per):
            at = pl.multiple_of((i * per + n) * LANES, LANES)
            parts = [summed[2 * n + j // 2][:, j % 2 * LANES : (j % 2 + 1) * LANES] for j in range(4)]
            for h in range(HEADS):
                o = parts[0][h * head : (h + 1) * head, :]
                total = parts[0][LANES : LANES + 1, :]
                for j in range(1, 4):
                    here = group_of == (h + j) % HEADS
                    o = jnp.where(here, parts[j][h * head : (h + 1) * head, :], o)
                    total = jnp.where(here[:1], parts[j][LANES : LANES + 1, :], total)
                o = (o * (1.0 / total)).astype(BF16)
                os[h * head : (h + 1) * head, pl.ds(at, LANES)] = turned(o, -h % HEADS)
        return carry

    lax.fori_loop(0, atoms // LANES // per, attend, 0)

    tall = 4096

    def finish(i, carry):
        at = pl.multiple_of(i * tall, tall)
        r = lax.dot_general(os[:, pl.ds(at, tall)], wout_ref[...], TN, preferred_element_type=F32)
        out_ref[pl.ds(at, tall), :] = (xs[pl.ds(at + PAD, tall), :].astype(F32) + r).astype(BF16)
        return carry

    lax.fori_loop(0, atoms // tall, finish, 0)

    acc[...] = jnp.zeros_like(acc)

    def pool(i, carry):
        parts = []
        for j in range(pgroup):
            at = pl.multiple_of((i * pgroup + j) * LANES, LANES)
            parts.append(
                lax.dot_general(
                    out_ref[pl.ds(at, LANES), :], member[pl.ds(at, LANES), :], TN, preferred_element_type=F32
                )
            )
        for j, part in enumerate(parts):
            to = pl.ds(pl.multiple_of(tiles_ref[0, i * pgroup + j] * LANES, LANES), 2 * LANES)
            acc[:, to] = acc[:, to] + part
        return carry

    lax.fori_loop(0, tiles // pgroup, pool, 0)
    send_a_ref[...] = acc[:, pl.ds(from_a, tok)].astype(BF16)
    send_b_ref[...] = acc[:, pl.ds(from_b, tok)].astype(BF16)
    mine_ref[...] = acc[:, base + tok : base + 2 * tok]


def shards(token_cond, atom_feat, atom_counts, w_token, w_query, w_key, w_value, w_out, w_back):
    tok = token_cond.shape[0]
    atoms, width = atom_feat.shape
    ndev = lax.axis_size("seq")

    def shifted(x, by):
        return lax.ppermute(x, "seq", [(i, (i + by) % ndev) for i in range(ndev)])

    counts = atom_counts.reshape(tok // LANES, LANES)
    copies = jnp.broadcast_to(counts, (ndev, *counts.shape))
    counts_all = lax.all_to_all(copies, "seq", split_axis=0, concat_axis=0, tiled=True)
    counts_all = counts_all.reshape(ndev * counts.shape[0], LANES)

    proj = jnp.dot(token_cond, w_token, preferred_element_type=F32).astype(BF16)
    ends = jnp.concatenate([proj, atom_feat[:PAD], atom_feat[atoms - PAD :]])
    ends, counts_all = lax.optimization_barrier((ends, counts_all))
    pairs_a = [(i, i ^ 1) for i in range(ndev)]
    pairs_b = [(i, ((i + 1) ^ 1) - 1) for i in range(1, ndev - 1)]
    near_a = lax.ppermute(ends, "seq", pairs_a)
    near_b = lax.ppermute(ends, "seq", pairs_b)
    whole = pl.BlockSpec(memory_space=pltpu.VMEM)

    chunks = 3 * tok // LANES
    near, far = pl.pallas_call(
        lambda *refs: plan_kernel(*refs, atoms=atoms, pad_chunks=1, chunks=chunks),
        out_shape=(
            jax.ShapeDtypeStruct((40, LANES), jnp.int32),
            jax.ShapeDtypeStruct((1, 1), jnp.int32),
        ),
        in_specs=[whole],
        out_specs=[whole] + [pl.BlockSpec(memory_space=pltpu.SMEM)],
        scratch_shapes=[pltpu.VMEM((counts_all.shape[0] + 16, LANES), jnp.int32)] * 2,
        compiler_params=pltpu.CompilerParams(vmem_limit_bytes=2 << 20),
        name="plan",
    )(counts_all)

    beyond = lax.cond(
        far[0, 0] > 0,
        lambda x: jnp.concatenate([shifted(x[tok - HALO :], 2), shifted(x[:HALO], -2)]),
        lambda x: jnp.zeros((2 * HALO, width), BF16),
        proj,
    )
    vmem = whole
    total = atoms + 2 * PAD
    window = jax.ShapeDtypeStruct((width, tok), BF16)
    atom_out, send_a, send_b, mine = pl.pallas_call(
        lambda *refs: atom_kernel(*refs, atoms=atoms, tok=tok, ndev=ndev),
        in_specs=[pl.BlockSpec(memory_space=pltpu.SMEM), pl.BlockSpec(memory_space=pl.ANY)] + [vmem] * 9,
        out_specs=[vmem] * 4,
        out_shape=(
            jax.ShapeDtypeStruct((atoms, width), BF16),
            window,
            window,
            jax.ShapeDtypeStruct((width, tok), F32),
        ),
        scratch_shapes=[
            pltpu.VMEM((3 * tok + 2 * LANES, width), BF16),
            pltpu.VMEM((atoms, 2 * LANES), BF16),
            pltpu.VMEM((total, width), BF16),
            pltpu.VMEM((width, atoms), BF16),
            pltpu.VMEM((total, width), BF16),
            pltpu.VMEM((width + ONES, total), BF16),
            pltpu.VMEM((width, atoms), BF16),
            pltpu.VMEM((width, 3 * tok + 2 * LANES), F32),
            pltpu.VMEM(near.shape, near.dtype),
            pltpu.SemaphoreType.DMA(()),
        ],
        compiler_params=pltpu.CompilerParams(vmem_limit_bytes=24 << 20),
        name="atoms",
    )(
        near, near, atom_feat, near_a, proj, near_b, beyond, w_query, w_key, w_value, w_out,
    )

    got_a = lax.ppermute(send_a, "seq", pairs_a)
    got_b = lax.ppermute(send_b, "seq", pairs_b)
    sums = mine + got_a.astype(F32) + got_b.astype(F32)
    pooled = (sums / atom_counts.astype(F32)[None, :]).astype(BF16)
    token_out = (
        token_cond.astype(F32) + lax.dot_general(pooled, w_back, TN, preferred_element_type=F32)
    ).astype(BF16)
    return (token_out, atom_out)


def solution(mesh):
    whole = P()
    rows = P(("batch", "seq"), None)
    in_specs = (rows, rows, P(("batch", "seq")), whole, whole, whole, whole, whole, whole)
    return jax.shard_map(shards, mesh=mesh, in_specs=in_specs, out_specs=(rows, rows), check_vma=False)
```

```python
import math

import jax
import jax.numpy as jnp
from jax import lax
from jax.experimental import pallas as pl
from jax.experimental.pallas import tpu as pltpu
from jax.sharding import PartitionSpec as P

BF16 = jnp.bfloat16
F32 = jnp.float32
HEADS = 4
QBLOCK = 32
KEYS = 128
HALO = 48
LANES = 128
ONES = 16
PAD = 64
NT = (((1,), (1,)), ((), ()))
TN = (((0,), (0,)), ((), ()))


def plan_kernel(counts_ref, near_ref, far_ref, spad, epad, *, atoms, pad_chunks, chunks):
    position = lax.axis_index("seq")
    rows = counts_ref.shape[0]
    counts = counts_ref[...].astype(F32)
    exact = counts.astype(BF16)
    up_to = (
        lax.broadcasted_iota(jnp.int32, (LANES, LANES), 0)
        <= lax.broadcasted_iota(jnp.int32, (LANES, LANES), 1)
    )
    within = jnp.dot(exact, up_to.astype(F32).astype(BF16), preferred_element_type=F32)
    before = (
        lax.broadcasted_iota(jnp.int32, (rows, rows), 1)
        < lax.broadcasted_iota(jnp.int32, (rows, rows), 0)
    )
    ahead = jnp.dot(before.astype(F32).astype(BF16), exact, preferred_element_type=F32)
    ends = (within + jnp.sum(ahead, axis=1, keepdims=True)).astype(jnp.int32) - position * atoms
    row = lax.broadcasted_iota(jnp.int32, (rows, LANES), 0) + 1
    lane = lax.broadcasted_iota(jnp.int32, (rows, LANES), 1)
    per_dev = chunks // 3
    drift = ends + position * atoms - row // per_dev * atoms
    closes = (row % per_dev == 0) & (lane == LANES - 1)
    wide = jnp.where(closes & (jnp.abs(drift) > atoms - HALO), 1.0, 0.0)
    far_ref[0, 0] = jnp.max(wide).astype(jnp.int32)
    far = 1 << 24
    spad[0:8, :] = jnp.full((8, LANES), -far, jnp.int32)
    epad[0:8, :] = jnp.full((8, LANES), -far, jnp.int32)
    spad[8 + rows : 16 + rows, :] = jnp.full((8, LANES), far, jnp.int32)
    epad[8 + rows : 16 + rows, :] = jnp.full((8, LANES), far, jnp.int32)
    spad[8 : 8 + rows, :] = ends - counts_ref[...]
    epad[8 : 8 + rows, :] = ends
    first = position * (chunks // 3) - (chunks // 3) - pad_chunks + 8
    near_ends = epad[pl.ds(first, 16), :]
    near_ref[8:24, :] = spad[pl.ds(first, 16), :]
    near_ref[24:, :] = near_ends
    lane = lax.broadcasted_iota(jnp.int32, (16, LANES), 1)
    row = lax.broadcasted_iota(jnp.int32, (16, LANES), 0)
    tiles = atoms // LANES
    tile_start = jnp.where(lane == tiles, -HALO, lane * LANES)
    tile_start = jnp.where(lane == tiles + 1, atoms, tile_start)
    total = chunks + 2 * pad_chunks
    passed = (near_ends[:, LANES - 1 :] <= tile_start) & (row < total)
    index = jnp.sum(passed.astype(F32), axis=0, keepdims=True).astype(jnp.int32)
    index = jnp.minimum(index, total - 2)
    near_ref[:8, :] = jnp.broadcast_to(index, (8, LANES))


def atom_kernel(
    tiles_ref, near_hbm, feat_ref, near_a_ref, own_ref, near_b_ref, far_ref,
    wq_ref, wk_ref, wv_ref, wout_ref,
    out_ref, send_a_ref, send_b_ref, mine_ref,
    table, member, xs, qx, ks, vs, os, acc, near_ref, near_sem,
    *, atoms, tok, ndev,
):
    position = lax.axis_index("seq")
    arrive = pltpu.make_async_copy(near_hbm, near_ref, near_sem)
    arrive.start()
    tiles = atoms // LANES
    edge = far_ref.shape[0] // 2
    zero = jnp.zeros((LANES - edge, LANES), BF16)
    base = LANES
    table[0 : base - edge, :] = zero
    table[base - edge : base, :] = far_ref[:edge, :]
    odd = lax.rem(position, 2)
    from_a = pl.multiple_of(base + (1 - odd) * 2 * tok, LANES)
    from_b = pl.multiple_of(base + odd * 2 * tok, LANES)
    table[pl.ds(from_a, tok), :] = near_a_ref[:tok, :]
    table[pl.ds(from_b, tok), :] = near_b_ref[:tok, :]
    table[base + tok : base + 2 * tok, :] = own_ref[...]
    table[base + 3 * tok : base + 3 * tok + edge, :] = far_ref[edge:, :]
    table[base + 3 * tok + edge :, :] = zero

    def members(chunk, first, height):
        ids = lax.broadcasted_iota(jnp.int32, (height, 2 * LANES), 0)
        lo = jnp.concatenate([near_ref[pl.ds(chunk + 8, 1), :], near_ref[pl.ds(chunk + 9, 1), :]], axis=1) - first
        hi = jnp.concatenate([near_ref[pl.ds(chunk + 24, 1), :], near_ref[pl.ds(chunk + 25, 1), :]], axis=1) - first
        return jnp.where((ids >= lo) & (ids < hi), 1.0, 0.0).astype(BF16)

    def rows_of(chunk, hit):
        window = table[pl.ds(pl.multiple_of(chunk * LANES, LANES), 2 * LANES), :]
        return jnp.dot(hit, window, preferred_element_type=F32)

    def halo_rows(index, first, feat):
        chunk = tiles_ref[0, index]
        got = rows_of(chunk, members(chunk, first, HALO))
        return (feat.astype(F32) + got).astype(BF16)

    is_odd = jnp.full((HALO, LANES), odd, jnp.int32) == 1
    before = slice(tok + 2 * PAD - HALO, tok + 2 * PAD)
    after = slice(tok, tok + HALO)
    arrive.wait()
    xs[0 : PAD - HALO, :] = jnp.zeros((PAD - HALO, LANES), BF16)
    xs[PAD + atoms + HALO :, :] = jnp.zeros((PAD - HALO, LANES), BF16)
    xs[PAD - HALO : PAD, :] = halo_rows(tiles, -HALO, jnp.where(is_odd, near_a_ref[before, :].astype(F32), near_b_ref[before, :].astype(F32)))
    xs[PAD + atoms : PAD + atoms + HALO, :] = halo_rows(tiles + 1, atoms, jnp.where(is_odd, near_b_ref[after, :].astype(F32), near_a_ref[after, :].astype(F32)))

    group = 32
    pgroup = 32

    def gather(i, carry):
        first = [pl.multiple_of((i * group + j) * LANES, LANES) for j in range(group)]
        chunk = [tiles_ref[0, i * group + j] for j in range(group)]
        hits = [members(c, at, LANES) for c, at in zip(chunk, first)]
        got = [rows_of(c, hit) for c, hit in zip(chunk, hits)]
        for at, hit, rows in zip(first, hits, got):
            member[pl.ds(at, LANES), :] = hit
            x = feat_ref[pl.ds(at, LANES), :].astype(F32) + rows
            xs[pl.ds(at + PAD, LANES), :] = x.astype(BF16)
        return carry

    lax.fori_loop(0, tiles // group, gather, 0)

    steps = 1
    span = (atoms + 2 * PAD) // steps
    broad = 4096
    wqt = wq_ref[...].T
    wvt = wv_ref[...].T

    def project(i, carry):
        at = pl.multiple_of(i * span, LANES)
        x = xs[pl.ds(at, span), :]
        ks[pl.ds(at, span), :] = jnp.dot(x, wk_ref[...], preferred_element_type=F32).astype(BF16)
        r = lax.dot_general(wvt, x, NT, preferred_element_type=F32).astype(BF16)
        vs[:LANES, pl.ds(at, span)] = r
        vs[LANES:, pl.ds(at, span)] = jnp.ones((ONES, span), BF16)
        return carry

    def turned(x, h):
        return pltpu.roll(x, h * QBLOCK % LANES, 1) if h % HEADS else x

    def ask(i, carry):
        at = pl.multiple_of(i * broad, LANES)
        r = lax.dot_general(wqt, xs[pl.ds(at + PAD, broad), :], NT, preferred_element_type=F32).astype(BF16)
        for c in range(broad // LANES):
            for h in range(HEADS):
                part = r[h * QBLOCK : (h + 1) * QBLOCK, c * LANES : (c + 1) * LANES]
                qx[h * QBLOCK : (h + 1) * QBLOCK, pl.ds(at + c * LANES, LANES)] = turned(part, h)
        return carry

    lax.fori_loop(0, steps, project, 0)
    lax.fori_loop(0, atoms // broad, ask, 0)

    lane = lax.broadcasted_iota(jnp.int32, vs.shape[:1] + (LANES,), 1)

    @pl.when(position == 0)
    def _():
        ks[PAD - HALO : PAD, :] = jnp.broadcast_to(ks[PAD : PAD + 1, :].astype(F32), (HALO, LANES)).astype(BF16)
        vs[:, :LANES] = jnp.where(lane < PAD, 0.0, vs[:, :LANES].astype(F32)).astype(BF16)

    @pl.when(position == ndev - 1)
    def _():
        last = PAD + atoms
        ks[last : last + HALO, :] = jnp.broadcast_to(ks[last - 1 : last, :].astype(F32), (HALO, LANES)).astype(BF16)
        vs[:, atoms:] = jnp.where(lane >= PAD, 0.0, vs[:, atoms:].astype(F32)).astype(BF16)

    head = LANES // HEADS
    scale = math.log2(math.e) / math.sqrt(head)
    row_group = lax.broadcasted_iota(jnp.int32, (LANES, LANES), 0) // head
    lane_group = lax.broadcasted_iota(jnp.int32, (LANES, LANES), 1) // QBLOCK
    kept = [((row_group + j) % HEADS == lane_group).astype(F32).astype(BF16) for j in range(4)]
    group_of = lax.broadcasted_iota(jnp.int32, (head, LANES), 1) // QBLOCK
    blank = jnp.zeros((LANES, LANES), BF16)

    per = 32

    def attend(i, carry):
        asked, weighed, summed = [], [], []
        for n in range(per):
            at = pl.multiple_of((i * per + n) * LANES, LANES)
            q = qx[:, pl.ds(at, LANES)]
            for j in (0, 2):
                key = [ks[pl.ds(at + PAD - HALO + (j + c) * QBLOCK, KEYS), :] for c in range(2)]
                ask_for = jnp.concatenate(
                    [
                        jnp.concatenate([q * kept[j], blank], axis=1),
                        jnp.concatenate([blank, q * kept[j + 1]], axis=1),
                    ],
                    axis=0,
                )
                asked.append(jnp.dot(jnp.concatenate(key, axis=1), ask_for, preferred_element_type=F32))
        for s in asked:
            top = jnp.max(s, axis=0, keepdims=True)
            weighed.append(jnp.exp2((s - top) * scale).astype(BF16))
        for n in range(per):
            at = pl.multiple_of((i * per + n) * LANES, LANES)
            value = vs[:, pl.ds(at, 2 * LANES)]
            for j in (0, 2):
                p = weighed[2 * n + j // 2]
                cols = []
                for c in range(2):
                    above = PAD - HALO + (j + c) * QBLOCK
                    cols.append(
                        jnp.concatenate(
                            [
                                jnp.zeros((above, LANES), BF16),
                                p[:, c * LANES : (c + 1) * LANES],
                                jnp.zeros((LANES - above, LANES), BF16),
                            ],
                            axis=0,
                        )
                    )
                summed.append(jnp.dot(value, jnp.concatenate(cols, axis=1), preferred_element_type=F32))
        for n in range(per):
            at = pl.multiple_of((i * per + n) * LANES, LANES)
            parts = [summed[2 * n + j // 2][:, j % 2 * LANES : (j % 2 + 1) * LANES] for j in range(4)]
            for h in range(HEADS):
                o = parts[0][h * head : (h + 1) * head, :]
                total = parts[0][LANES : LANES + 1, :]
                for j in range(1, 4):
                    here = group_of == (h + j) % HEADS
                    o = jnp.where(here, parts[j][h * head : (h + 1) * head, :], o)
                    total = jnp.where(here[:1], parts[j][LANES : LANES + 1, :], total)
                o = (o * (1.0 / total)).astype(BF16)
                os[h * head : (h + 1) * head, pl.ds(at, LANES)] = turned(o, -h % HEADS)
        return carry

    lax.fori_loop(0, atoms // LANES // per, attend, 0)

    tall = 4096

    def finish(i, carry):
        at = pl.multiple_of(i * tall, tall)
        r = lax.dot_general(os[:, pl.ds(at, tall)], wout_ref[...], TN, preferred_element_type=F32)
        out_ref[pl.ds(at, tall), :] = (xs[pl.ds(at + PAD, tall), :].astype(F32) + r).astype(BF16)
        return carry

    lax.fori_loop(0, atoms // tall, finish, 0)

    acc[...] = jnp.zeros_like(acc)

    def pool(i, carry):
        parts = []
        for j in range(pgroup):
            at = pl.multiple_of((i * pgroup + j) * LANES, LANES)
            parts.append(
                lax.dot_general(
                    out_ref[pl.ds(at, LANES), :], member[pl.ds(at, LANES), :], TN, preferred_element_type=F32
                )
            )
        for j, part in enumerate(parts):
            to = pl.ds(pl.multiple_of(tiles_ref[0, i * pgroup + j] * LANES, LANES), 2 * LANES)
            acc[:, to] = acc[:, to] + part
        return carry

    lax.fori_loop(0, tiles // pgroup, pool, 0)
    send_a_ref[...] = acc[:, pl.ds(from_a, tok)].astype(BF16)
    send_b_ref[...] = acc[:, pl.ds(from_b, tok)].astype(BF16)
    mine_ref[...] = acc[:, base + tok : base + 2 * tok]


def shards(token_cond, atom_feat, atom_counts, w_token, w_query, w_key, w_value, w_out, w_back):
    tok = token_cond.shape[0]
    atoms, width = atom_feat.shape
    ndev = lax.axis_size("seq")

    def shifted(x, by):
        return lax.ppermute(x, "seq", [(i, (i + by) % ndev) for i in range(ndev)])

    counts = atom_counts.reshape(tok // LANES, LANES)
    copies = jnp.broadcast_to(counts, (ndev, *counts.shape))
    counts_all = lax.all_to_all(copies, "seq", split_axis=0, concat_axis=0, tiled=True)
    counts_all = counts_all.reshape(ndev * counts.shape[0], LANES)

    proj = jnp.dot(token_cond, w_token, preferred_element_type=F32).astype(BF16)
    ends = jnp.concatenate([proj, atom_feat[:PAD], atom_feat[atoms - PAD :]])
    ends, counts_all = lax.optimization_barrier((ends, counts_all))
    pairs_a = [(i, i ^ 1) for i in range(ndev)]
    pairs_b = [
        (
            part * ndev + i,
            part * ndev + ((i + 1) ^ 1) - 1 if 0 < i < ndev - 1 else (part ^ 1) * ndev + i,
        )
        for part in range(lax.axis_size("batch"))
        for i in range(ndev)
    ]
    near_a = lax.ppermute(ends, "seq", pairs_a)
    near_b = lax.ppermute(ends, ("batch", "seq"), pairs_b)
    whole = pl.BlockSpec(memory_space=pltpu.VMEM)

    chunks = 3 * tok // LANES
    near, far = pl.pallas_call(
        lambda *refs: plan_kernel(*refs, atoms=atoms, pad_chunks=1, chunks=chunks),
        out_shape=(
            jax.ShapeDtypeStruct((40, LANES), jnp.int32),
            jax.ShapeDtypeStruct((1, 1), jnp.int32),
        ),
        in_specs=[whole],
        out_specs=[whole] + [pl.BlockSpec(memory_space=pltpu.SMEM)],
        scratch_shapes=[pltpu.VMEM((counts_all.shape[0] + 16, LANES), jnp.int32)] * 2,
        compiler_params=pltpu.CompilerParams(vmem_limit_bytes=2 << 20),
        name="plan",
    )(counts_all)

    beyond = lax.cond(
        far[0, 0] > 0,
        lambda x: jnp.concatenate([shifted(x[tok - HALO :], 2), shifted(x[:HALO], -2)]),
        lambda x: jnp.zeros((2 * HALO, width), BF16),
        proj,
    )
    vmem = whole
    total = atoms + 2 * PAD
    window = jax.ShapeDtypeStruct((width, tok), BF16)
    atom_out, send_a, send_b, mine = pl.pallas_call(
        lambda *refs: atom_kernel(*refs, atoms=atoms, tok=tok, ndev=ndev),
        in_specs=[pl.BlockSpec(memory_space=pltpu.SMEM), pl.BlockSpec(memory_space=pl.ANY)] + [vmem] * 9,
        out_specs=[vmem] * 4,
        out_shape=(
            jax.ShapeDtypeStruct((atoms, width), BF16),
            window,
            window,
            jax.ShapeDtypeStruct((width, tok), F32),
        ),
        scratch_shapes=[
            pltpu.VMEM((3 * tok + 2 * LANES, width), BF16),
            pltpu.VMEM((atoms, 2 * LANES), BF16),
            pltpu.VMEM((total, width), BF16),
            pltpu.VMEM((width, atoms), BF16),
            pltpu.VMEM((total, width), BF16),
            pltpu.VMEM((width + ONES, total), BF16),
            pltpu.VMEM((width, atoms), BF16),
            pltpu.VMEM((width, 3 * tok + 2 * LANES), F32),
            pltpu.VMEM(near.shape, near.dtype),
            pltpu.SemaphoreType.DMA(()),
        ],
        compiler_params=pltpu.CompilerParams(vmem_limit_bytes=24 << 20),
        name="atoms",
    )(
        near, near, atom_feat, near_a, proj, near_b, beyond, w_query, w_key, w_value, w_out,
    )

    got_a = lax.ppermute(send_a, "seq", pairs_a)
    got_b = lax.ppermute(send_b, ("batch", "seq"), pairs_b)
    sums = mine + got_a.astype(F32) + got_b.astype(F32)
    pooled = (sums / atom_counts.astype(F32)[None, :]).astype(BF16)
    token_out = (
        token_cond.astype(F32) + lax.dot_general(pooled, w_back, TN, preferred_element_type=F32)
    ).astype(BF16)
    return (token_out, atom_out)


def solution(mesh):
    whole = P()
    rows = P(("batch", "seq"), None)
    in_specs = (rows, rows, P(("batch", "seq")), whole, whole, whole, whole, whole, whole)
    return jax.shard_map(shards, mesh=mesh, in_specs=in_specs, out_specs=(rows, rows), check_vma=False)
```

```python
import math

import jax
import jax.numpy as jnp
from jax import lax
from jax.experimental import pallas as pl
from jax.experimental.pallas import tpu as pltpu
from jax.sharding import PartitionSpec as P

BF16 = jnp.bfloat16
F32 = jnp.float32
HEADS = 4
QBLOCK = 32
KEYS = 128
HALO = 48
LANES = 128
ONES = 16
PAD = 64
NT = (((1,), (1,)), ((), ()))
TN = (((0,), (0,)), ((), ()))


def plan_kernel(counts_ref, near_ref, far_ref, spad, epad, *, atoms, pad_chunks, chunks):
    position = lax.axis_index("seq")
    rows = counts_ref.shape[0]
    counts = counts_ref[...].astype(F32)
    exact = counts.astype(BF16)
    up_to = (
        lax.broadcasted_iota(jnp.int32, (LANES, LANES), 0)
        <= lax.broadcasted_iota(jnp.int32, (LANES, LANES), 1)
    )
    within = jnp.dot(exact, up_to.astype(F32).astype(BF16), preferred_element_type=F32)
    before = (
        lax.broadcasted_iota(jnp.int32, (rows, rows), 1)
        < lax.broadcasted_iota(jnp.int32, (rows, rows), 0)
    )
    ahead = jnp.dot(before.astype(F32).astype(BF16), exact, preferred_element_type=F32)
    ends = (within + jnp.sum(ahead, axis=1, keepdims=True)).astype(jnp.int32) - position * atoms
    row = lax.broadcasted_iota(jnp.int32, (rows, LANES), 0) + 1
    lane = lax.broadcasted_iota(jnp.int32, (rows, LANES), 1)
    per_dev = chunks // 3
    drift = ends + position * atoms - row // per_dev * atoms
    closes = (row % per_dev == 0) & (lane == LANES - 1)
    wide = jnp.where(closes & (jnp.abs(drift) > atoms - HALO), 1.0, 0.0)
    far_ref[0, 0] = jnp.max(wide).astype(jnp.int32)
    far = 1 << 24
    spad[0:8, :] = jnp.full((8, LANES), -far, jnp.int32)
    epad[0:8, :] = jnp.full((8, LANES), -far, jnp.int32)
    spad[8 + rows : 16 + rows, :] = jnp.full((8, LANES), far, jnp.int32)
    epad[8 + rows : 16 + rows, :] = jnp.full((8, LANES), far, jnp.int32)
    spad[8 : 8 + rows, :] = ends - counts_ref[...]
    epad[8 : 8 + rows, :] = ends
    first = position * (chunks // 3) - (chunks // 3) - pad_chunks + 8
    near_ends = epad[pl.ds(first, 16), :]
    near_ref[8:24, :] = spad[pl.ds(first, 16), :]
    near_ref[24:, :] = near_ends
    lane = lax.broadcasted_iota(jnp.int32, (16, LANES), 1)
    row = lax.broadcasted_iota(jnp.int32, (16, LANES), 0)
    tiles = atoms // LANES
    tile_start = jnp.where(lane == tiles, -HALO, lane * LANES)
    tile_start = jnp.where(lane == tiles + 1, atoms, tile_start)
    total = chunks + 2 * pad_chunks
    passed = (near_ends[:, LANES - 1 :] <= tile_start) & (row < total)
    index = jnp.sum(passed.astype(F32), axis=0, keepdims=True).astype(jnp.int32)
    index = jnp.minimum(index, total - 2)
    near_ref[:8, :] = jnp.broadcast_to(index, (8, LANES))


def atom_kernel(
    tiles_ref, near_hbm, feat_ref, near_a_ref, own_ref, near_b_ref, far_ref,
    wq_ref, wk_ref, wv_ref, wout_ref,
    out_ref, send_a_ref, send_b_ref, mine_ref,
    table, member, xs, qx, ks, vs, os, acc, near_ref, near_sem,
    *, atoms, tok, ndev,
):
    position = lax.axis_index("seq")
    arrive = pltpu.make_async_copy(near_hbm, near_ref, near_sem)
    arrive.start()
    tiles = atoms // LANES
    edge = far_ref.shape[0] // 2
    zero = jnp.zeros((LANES - edge, LANES), BF16)
    base = LANES
    table[0 : base - edge, :] = zero
    table[base - edge : base, :] = far_ref[:edge, :]
    odd = lax.rem(position, 2)
    from_a = pl.multiple_of(base + (1 - odd) * 2 * tok, LANES)
    from_b = pl.multiple_of(base + odd * 2 * tok, LANES)
    table[pl.ds(from_a, tok), :] = near_a_ref[:tok, :]
    table[pl.ds(from_b, tok), :] = near_b_ref[:tok, :]
    table[base + tok : base + 2 * tok, :] = own_ref[...]
    table[base + 3 * tok : base + 3 * tok + edge, :] = far_ref[edge:, :]
    table[base + 3 * tok + edge :, :] = zero

    def members(chunk, first, height):
        ids = lax.broadcasted_iota(jnp.int32, (height, 2 * LANES), 0)
        lo = jnp.concatenate([near_ref[pl.ds(chunk + 8, 1), :], near_ref[pl.ds(chunk + 9, 1), :]], axis=1) - first
        hi = jnp.concatenate([near_ref[pl.ds(chunk + 24, 1), :], near_ref[pl.ds(chunk + 25, 1), :]], axis=1) - first
        return jnp.where((ids >= lo) & (ids < hi), 1.0, 0.0).astype(BF16)

    def rows_of(chunk, hit):
        window = table[pl.ds(pl.multiple_of(chunk * LANES, LANES), 2 * LANES), :]
        return jnp.dot(hit, window, preferred_element_type=F32)

    def halo_rows(index, first, feat):
        chunk = tiles_ref[0, index]
        got = rows_of(chunk, members(chunk, first, HALO))
        return (feat.astype(F32) + got).astype(BF16)

    is_odd = jnp.full((HALO, LANES), odd, jnp.int32) == 1
    before = slice(tok + 2 * PAD - HALO, tok + 2 * PAD)
    after = slice(tok, tok + HALO)
    arrive.wait()
    xs[0 : PAD - HALO, :] = jnp.zeros((PAD - HALO, LANES), BF16)
    xs[PAD + atoms + HALO :, :] = jnp.zeros((PAD - HALO, LANES), BF16)
    xs[PAD - HALO : PAD, :] = halo_rows(tiles, -HALO, jnp.where(is_odd, near_a_ref[before, :].astype(F32), near_b_ref[before, :].astype(F32)))
    xs[PAD + atoms : PAD + atoms + HALO, :] = halo_rows(tiles + 1, atoms, jnp.where(is_odd, near_b_ref[after, :].astype(F32), near_a_ref[after, :].astype(F32)))

    group = 32
    pgroup = 32

    def gather(i, carry):
        first = [pl.multiple_of((i * group + j) * LANES, LANES) for j in range(group)]
        chunk = [tiles_ref[0, i * group + j] for j in range(group)]
        hits = [members(c, at, LANES) for c, at in zip(chunk, first)]
        got = [rows_of(c, hit) for c, hit in zip(chunk, hits)]
        for at, hit, rows in zip(first, hits, got):
            member[pl.ds(at, LANES), :] = hit
            x = feat_ref[pl.ds(at, LANES), :].astype(F32) + rows
            xs[pl.ds(at + PAD, LANES), :] = x.astype(BF16)
        return carry

    lax.fori_loop(0, tiles // group, gather, 0)

    steps = 1
    span = (atoms + 2 * PAD) // steps
    broad = 4096
    wqt = wq_ref[...].T
    wvt = wv_ref[...].T

    def project(i, carry):
        at = pl.multiple_of(i * span, LANES)
        x = xs[pl.ds(at, span), :]
        ks[pl.ds(at, span), :] = jnp.dot(x, wk_ref[...], preferred_element_type=F32).astype(BF16)
        r = lax.dot_general(wvt, x, NT, preferred_element_type=F32).astype(BF16)
        vs[:LANES, pl.ds(at, span)] = r
        vs[LANES:, pl.ds(at, span)] = jnp.ones((ONES, span), BF16)
        return carry

    def turned(x, h):
        return pltpu.roll(x, h * QBLOCK % LANES, 1) if h % HEADS else x

    def ask(i, carry):
        at = pl.multiple_of(i * broad, LANES)
        r = lax.dot_general(wqt, xs[pl.ds(at + PAD, broad), :], NT, preferred_element_type=F32).astype(BF16)
        for c in range(broad // LANES):
            for h in range(HEADS):
                part = r[h * QBLOCK : (h + 1) * QBLOCK, c * LANES : (c + 1) * LANES]
                qx[h * QBLOCK : (h + 1) * QBLOCK, pl.ds(at + c * LANES, LANES)] = turned(part, h)
        return carry

    lax.fori_loop(0, steps, project, 0)
    lax.fori_loop(0, atoms // broad, ask, 0)

    lane = lax.broadcasted_iota(jnp.int32, vs.shape[:1] + (LANES,), 1)

    @pl.when(position == 0)
    def _():
        ks[PAD - HALO : PAD, :] = jnp.broadcast_to(ks[PAD : PAD + 1, :].astype(F32), (HALO, LANES)).astype(BF16)
        vs[:, :LANES] = jnp.where(lane < PAD, 0.0, vs[:, :LANES].astype(F32)).astype(BF16)

    @pl.when(position == ndev - 1)
    def _():
        last = PAD + atoms
        ks[last : last + HALO, :] = jnp.broadcast_to(ks[last - 1 : last, :].astype(F32), (HALO, LANES)).astype(BF16)
        vs[:, atoms:] = jnp.where(lane >= PAD, 0.0, vs[:, atoms:].astype(F32)).astype(BF16)

    head = LANES // HEADS
    scale = math.log2(math.e) / math.sqrt(head)
    row_group = lax.broadcasted_iota(jnp.int32, (LANES, LANES), 0) // head
    lane_group = lax.broadcasted_iota(jnp.int32, (LANES, LANES), 1) // QBLOCK
    kept = [((row_group + j) % HEADS == lane_group).astype(F32).astype(BF16) for j in range(4)]
    group_of = lax.broadcasted_iota(jnp.int32, (head, LANES), 1) // QBLOCK
    blank = jnp.zeros((LANES, LANES), BF16)

    per = 32

    def attend(i, carry):
        asked, weighed, summed = [], [], []
        for n in range(per):
            at = pl.multiple_of((i * per + n) * LANES, LANES)
            q = qx[:, pl.ds(at, LANES)]
            for j in (0, 2):
                key = [ks[pl.ds(at + PAD - HALO + (j + c) * QBLOCK, KEYS), :] for c in range(2)]
                ask_for = jnp.concatenate(
                    [
                        jnp.concatenate([q * kept[j], blank], axis=1),
                        jnp.concatenate([blank, q * kept[j + 1]], axis=1),
                    ],
                    axis=0,
                )
                asked.append(jnp.dot(jnp.concatenate(key, axis=1), ask_for, preferred_element_type=F32))
        for s in asked:
            top = jnp.max(s, axis=0, keepdims=True)
            weighed.append(jnp.exp2((s - top) * scale).astype(BF16))
        for n in range(per):
            at = pl.multiple_of((i * per + n) * LANES, LANES)
            value = vs[:, pl.ds(at, 2 * LANES)]
            for j in (0, 2):
                p = weighed[2 * n + j // 2]
                cols = []
                for c in range(2):
                    above = PAD - HALO + (j + c) * QBLOCK
                    cols.append(
                        jnp.concatenate(
                            [
                                jnp.zeros((above, LANES), BF16),
                                p[:, c * LANES : (c + 1) * LANES],
                                jnp.zeros((LANES - above, LANES), BF16),
                            ],
                            axis=0,
                        )
                    )
                summed.append(jnp.dot(value, jnp.concatenate(cols, axis=1), preferred_element_type=F32))
        for n in range(per):
            at = pl.multiple_of((i * per + n) * LANES, LANES)
            parts = [summed[2 * n + j // 2][:, j % 2 * LANES : (j % 2 + 1) * LANES] for j in range(4)]
            for h in range(HEADS):
                o = parts[0][h * head : (h + 1) * head, :]
                total = parts[0][LANES : LANES + 1, :]
                for j in range(1, 4):
                    here = group_of == (h + j) % HEADS
                    o = jnp.where(here, parts[j][h * head : (h + 1) * head, :], o)
                    total = jnp.where(here[:1], parts[j][LANES : LANES + 1, :], total)
                o = (o * (1.0 / total)).astype(BF16)
                os[h * head : (h + 1) * head, pl.ds(at, LANES)] = turned(o, -h % HEADS)
        return carry

    lax.fori_loop(0, atoms // LANES // per, attend, 0)

    tall = 4096

    def finish(i, carry):
        at = pl.multiple_of(i * tall, tall)
        r = lax.dot_general(os[:, pl.ds(at, tall)], wout_ref[...], TN, preferred_element_type=F32)
        out_ref[pl.ds(at, tall), :] = (xs[pl.ds(at + PAD, tall), :].astype(F32) + r).astype(BF16)
        return carry

    lax.fori_loop(0, atoms // tall, finish, 0)

    acc[...] = jnp.zeros_like(acc)

    def pool(i, carry):
        parts = []
        for j in range(pgroup):
            at = pl.multiple_of((i * pgroup + j) * LANES, LANES)
            parts.append(
                lax.dot_general(
                    out_ref[pl.ds(at, LANES), :], member[pl.ds(at, LANES), :], TN, preferred_element_type=F32
                )
            )
        for j, part in enumerate(parts):
            to = pl.ds(pl.multiple_of(tiles_ref[0, i * pgroup + j] * LANES, LANES), 2 * LANES)
            acc[:, to] = acc[:, to] + part
        return carry

    lax.fori_loop(0, tiles // pgroup, pool, 0)
    send_a_ref[...] = acc[:, pl.ds(from_a, tok)].astype(BF16)
    send_b_ref[...] = acc[:, pl.ds(from_b, tok)].astype(BF16)
    mine_ref[...] = acc[:, base + tok : base + 2 * tok]


def shards(token_cond, atom_feat, atom_counts, w_token, w_query, w_key, w_value, w_out, w_back):
    tok = token_cond.shape[0]
    atoms, width = atom_feat.shape
    ndev = lax.axis_size("seq")

    def shifted(x, by):
        return lax.ppermute(x, "seq", [(i, (i + by) % ndev) for i in range(ndev)])

    counts = atom_counts.reshape(tok // LANES, LANES)
    copies = jnp.broadcast_to(counts, (ndev, *counts.shape))
    counts_all = lax.all_to_all(copies, "seq", split_axis=0, concat_axis=0, tiled=True)
    counts_all = counts_all.reshape(ndev * counts.shape[0], LANES)

    proj = jnp.dot(token_cond, w_token, preferred_element_type=F32).astype(BF16)
    ends = jnp.concatenate([proj, atom_feat[:PAD], atom_feat[atoms - PAD :]])
    pairs_a = [(i, i ^ 1) for i in range(ndev)]
    pairs_b = [
        (
            part * ndev + i,
            part * ndev + ((i + 1) ^ 1) - 1 if 0 < i < ndev - 1 else (part ^ 1) * ndev + i,
        )
        for part in range(lax.axis_size("batch"))
        for i in range(ndev)
    ]
    near_a = lax.ppermute(ends, "seq", pairs_a)
    near_b = lax.ppermute(ends, ("batch", "seq"), pairs_b)
    whole = pl.BlockSpec(memory_space=pltpu.VMEM)

    chunks = 3 * tok // LANES
    near, far = pl.pallas_call(
        lambda *refs: plan_kernel(*refs, atoms=atoms, pad_chunks=1, chunks=chunks),
        out_shape=(
            jax.ShapeDtypeStruct((40, LANES), jnp.int32),
            jax.ShapeDtypeStruct((1, 1), jnp.int32),
        ),
        in_specs=[whole],
        out_specs=[whole] + [pl.BlockSpec(memory_space=pltpu.SMEM)],
        scratch_shapes=[pltpu.VMEM((counts_all.shape[0] + 16, LANES), jnp.int32)] * 2,
        compiler_params=pltpu.CompilerParams(vmem_limit_bytes=2 << 20),
        name="plan",
    )(counts_all)

    beyond = lax.cond(
        far[0, 0] > 0,
        lambda x: jnp.concatenate([shifted(x[tok - HALO :], 2), shifted(x[:HALO], -2)]),
        lambda x: jnp.zeros((2 * HALO, width), BF16),
        proj,
    )
    vmem = whole
    total = atoms + 2 * PAD
    window = jax.ShapeDtypeStruct((width, tok), BF16)
    atom_out, send_a, send_b, mine = pl.pallas_call(
        lambda *refs: atom_kernel(*refs, atoms=atoms, tok=tok, ndev=ndev),
        in_specs=[pl.BlockSpec(memory_space=pltpu.SMEM), pl.BlockSpec(memory_space=pl.ANY)] + [vmem] * 9,
        out_specs=[vmem] * 4,
        out_shape=(
            jax.ShapeDtypeStruct((atoms, width), BF16),
            window,
            window,
            jax.ShapeDtypeStruct((width, tok), F32),
        ),
        scratch_shapes=[
            pltpu.VMEM((3 * tok + 2 * LANES, width), BF16),
            pltpu.VMEM((atoms, 2 * LANES), BF16),
            pltpu.VMEM((total, width), BF16),
            pltpu.VMEM((width, atoms), BF16),
            pltpu.VMEM((total, width), BF16),
            pltpu.VMEM((width + ONES, total), BF16),
            pltpu.VMEM((width, atoms), BF16),
            pltpu.VMEM((width, 3 * tok + 2 * LANES), F32),
            pltpu.VMEM(near.shape, near.dtype),
            pltpu.SemaphoreType.DMA(()),
        ],
        compiler_params=pltpu.CompilerParams(vmem_limit_bytes=24 << 20),
        name="atoms",
    )(
        near, near, atom_feat, near_a, proj, near_b, beyond, w_query, w_key, w_value, w_out,
    )

    got_a = lax.ppermute(send_a, "seq", pairs_a)
    got_b = lax.ppermute(send_b, ("batch", "seq"), pairs_b)
    sums = mine + got_a.astype(F32) + got_b.astype(F32)
    pooled = (sums / atom_counts.astype(F32)[None, :]).astype(BF16)
    token_out = (
        token_cond.astype(F32) + lax.dot_general(pooled, w_back, TN, preferred_element_type=F32)
    ).astype(BF16)
    return (token_out, atom_out)


def solution(mesh):
    whole = P()
    rows = P(("batch", "seq"), None)
    in_specs = (rows, rows, P(("batch", "seq")), whole, whole, whole, whole, whole, whole)
    return jax.shard_map(shards, mesh=mesh, in_specs=in_specs, out_specs=(rows, rows), check_vma=False)
```
